256 devices in a mesh: chain: 4 (over y), row: 64 (over x, z, core).
Axes of the slice: x: 4, y: 4, z: 8, core: 2. Of those that a mesh axis runs over, the one named last changes fastest.
Arguments:
- right_side: float32 [131072, 128], P('row'), may hold values from -6 to 6
- factor: bfloat16 [131072, 1, 2048], P('row', None, 'chain'), may hold values from -0.125 to 0.125
- tile_scales: float32 [256, 1, 4], P('row', None, 'chain'), may hold values from 0.5 to 2
- diag_inverse: float32 [1, 512, 2048], P(None, None, 'chain'), may hold values from -0.25 to 0.25
Outputs:
- updated: float32 [131072, 128], P('row')
The draws below stay inside these ranges and needn't reach their ends.
All inputs are finite; a program needn't handle non-finite values.
Results may differ from the reference program's by a relative error of at most 0.0031.
Values may be sent and summed in bfloat16 or wider, within the bound.
No kernel may reach another device: no remote copies, remote signals or barrier semaphores. Data moves between devices by JAX's collectives and lax.ppermute only.
A program may use at most 64 MiB of HBM per device.

```python
import math
import jax
import jax.numpy as jnp
from jax import lax

N = 131072
RHS = 128
NB = 512
ROUNDS = 1
WINDOW = 2048
CHAIN_COLS = 2048
N_CHAIN = 4


def level_of(key, extent, cuts, low, largest):
    gain, own = 1.0, jax.random.fold_in(key, 6)
    for axis_at, shards_of in cuts:
        draws = jnp.exp(jax.random.uniform(jax.random.fold_in(own, axis_at), (shards_of,), jnp.float32, low / len(cuts), largest / len(cuts)))
        gain = gain * jnp.repeat(draws, extent[axis_at] // shards_of).reshape([-1 if axis == axis_at else 1 for axis in range(len(extent))])
    return gain


def gaussian(own_key, dims, spread, limit, cuts=(), kind=jnp.bfloat16):
    array = spread * jax.random.normal(own_key, dims, jnp.float32)
    if cuts:
        array = array * level_of(own_key, dims, cuts, -0.22, 0.18)
    return jnp.clip(array, -limit, limit).astype(kind)


def setup_inputs(seed: int = 0) -> dict:
    keys = jax.random.split(jax.random.key(seed), 5)
    return {
        "right_side": gaussian(keys[0], (N, RHS), 1.0, 6.0, ((0, 64),), jnp.float32),
        "factor": gaussian(keys[1], (N, ROUNDS, CHAIN_COLS), WINDOW ** -0.5, 0.125, ((0, 64), (2, 4))),
        "tile_scales": jnp.clip(jnp.exp(math.log(2.0) - 1.3862944 * jax.random.uniform(keys[2], (N // NB, ROUNDS, N_CHAIN), jnp.float32) ** level_of(keys[2], (N // NB, ROUNDS, N_CHAIN), ((0, 64), (2, 4)), -0.2, 0.2)), 0.5, 2.0),
        "diag_inverse": gaussian(keys[3], (ROUNDS, NB, CHAIN_COLS), NB ** -0.5, 0.25, ((2, 4),), jnp.float32),
    }


def reference(right_side, factor, tile_scales, diag_inverse):
    row_count, rhs_count = right_side.shape
    block_count = ROUNDS * N_CHAIN
    window = block_count * NB
    row_ids = jnp.arange(row_count, dtype=jnp.int32)
    zero = jnp.int32(0)

    def step(column, carry):
        carried, solved = carry
        column = jnp.asarray(column).astype(jnp.int32)
        round_index = column // N_CHAIN
        chain_slot = column % N_CHAIN
        block_start = column * NB
        residue = lax.dynamic_slice(right_side, (block_start, zero), (NB, rhs_count)) - lax.dynamic_slice(carried, (block_start, zero), (NB, rhs_count))
        inverse = lax.dynamic_slice(diag_inverse, (round_index, zero, chain_slot * NB), (1, NB, NB))[0]
        solved_now = jnp.dot(inverse, residue, precision=lax.Precision.HIGHEST, preferred_element_type=jnp.float32)
        solved_low = solved_now.astype(jnp.bfloat16)
        panel = lax.dynamic_slice(factor, (zero, round_index, chain_slot * NB), (row_count, 1, NB))[:, 0, :]
        product = jnp.dot(panel.astype(jnp.float32), solved_low.astype(jnp.float32), precision=lax.Precision.HIGHEST, preferred_element_type=jnp.float32)
        tile_scale = lax.dynamic_slice(tile_scales, (zero, round_index, chain_slot), (row_count // NB, 1, 1))[:, 0, 0]
        product = (product.reshape(row_count // NB, NB, rhs_count) * tile_scale[:, None, None]).reshape(row_count, rhs_count)
        below = row_ids >= block_start + NB
        carried = carried + jnp.where(below[:, None], product, jnp.zeros_like(product))
        solved = lax.dynamic_update_slice(solved, solved_now, (block_start, zero))
        return carried, solved

    carried = jnp.zeros((row_count, rhs_count), jnp.float32)
    solved = jnp.zeros((window, rhs_count), jnp.float32)
    carried, solved = lax.fori_loop(0, block_count, step, (carried, solved))
    tail = right_side[window:] - carried[window:]
    return jnp.concatenate([solved, tail], axis=0)
```

```python
import jax
import jax.numpy as jnp
from jax import lax
from jax.experimental import pallas as pl
from jax.experimental.pallas import tpu as pltpu
from jax.sharding import PartitionSpec as P


BF16 = jnp.bfloat16
F32 = jnp.float32
BLOCK = 512
RHS = 128
CHAINS = 4
ROWS = 64
CHUNKS = 4
KERNEL_VMEM = 12 * 1024 * 1024

TREE = {
    (0, 0): ((0, 7), (1, 0), (1, 7), (3, 0), (3, 7)),
    (2, 1): ((1, 1), (2, 0), (2, 2), (3, 1)),
    (1, 3): ((0, 3), (1, 4), (2, 3), (2, 4)),
    (2, 6): ((1, 6), (2, 5), (2, 7), (3, 6)),
    (0, 2): ((0, 1), (1, 2), (3, 2), (3, 3)),
    (0, 5): ((0, 4), (0, 6), (1, 5), (3, 4), (3, 5)),
}
CENTRES = tuple(TREE)
RELAY = (0, 2)
CORE_PAIRS = [[2 * i, 2 * i + 1] for i in range(ROWS // 2)]

VMEM = pl.BlockSpec(memory_space=pltpu.VMEM)
HBM = pl.BlockSpec(memory_space=pltpu.HBM)
COLUMN = pltpu.VMEM((BLOCK, RHS), F32)
LOW = pltpu.VMEM((BLOCK, RHS), BF16)


def row_of(chip, core=0):
    return chip[0] * 16 + chip[1] * 2 + core


def device_of(chain, chip, core=0):
    return chain * ROWS + row_of(chip, core)


def fan_out(tree):
    rounds = max((len(leaves) + 1) // 2 for leaves in tree.values())
    steps = [[] for _ in range(rounds)]
    for chip, leaves in tree.items():
        for i, leaf in enumerate(leaves):
            steps[i // 2].append((chip, i % 2, leaf))
    return steps


def on_chip(value):
    return pltpu.with_memory_space_constraint(value, pltpu.VMEM)


def call(body, outs, specs, *args, scratch=()):
    args = [
        pltpu.with_memory_space_constraint(a, s.memory_space) for a, s in zip(args, specs)
    ]
    single = not isinstance(outs, tuple)
    return pl.pallas_call(
        body,
        out_shape=outs,
        in_specs=specs,
        out_specs=VMEM if single else (VMEM,) * len(outs),
        scratch_shapes=scratch,
        compiler_params=pltpu.CompilerParams(vmem_limit_bytes=KERNEL_VMEM),
    )(*args)


def dot(a, b):
    return jnp.dot(a, b, preferred_element_type=F32)


def split(value):
    high = value.astype(BF16)
    return high, (value - high.astype(F32)).astype(BF16)


def product(high_ref, low_ref, value):
    high, low = split(value)
    return dot(high_ref[...], high) + dot(high_ref[...], low) + dot(low_ref[...], high)


def chain_index():
    return lax.axis_index("chain")


def is_head():
    return lax.axis_index("row") == 0


def block(i):
    return pl.ds(pl.multiple_of(i * BLOCK, BLOCK), BLOCK)


def own(ref):
    return ref[block(chain_index()), :]


def tile(scales, panel, i, solved_low):
    return scales[i : i + 1, :] * dot(panel[i * BLOCK : (i + 1) * BLOCK, :], solved_low)


def first(
    scales_in, rhs_in, inverse_in, panel_in, rhs, panel, high, low, scales, u1, u23, inverse, mine, numbers, sems
):
    chunk = BLOCK // CHUNKS
    parts = [pl.ds(i * chunk, chunk) for i in range(CHUNKS)]
    tiles = [pl.ds(i * BLOCK, BLOCK) for i in range(CHAINS)]
    here = block(chain_index())

    def copies(source, target, slices, at):
        return [
            pltpu.make_async_copy(source.at[rows], target.at[rows], sems.at[at + n])
            for n, rows in enumerate(slices)
        ]

    scale_load = pltpu.make_async_copy(scales_in, numbers, sems.at[0])
    own_load = pltpu.make_async_copy(rhs_in.at[here, :], mine, sems.at[1])
    inverse_loads = copies(inverse_in, inverse, parts, 2)
    panel_loads = copies(panel_in, panel, tiles, 2 + CHUNKS)
    rhs_load = pltpu.make_async_copy(rhs_in, rhs, sems.at[2 + CHUNKS + CHAINS])
    own_load.start()
    for load in inverse_loads:
        load.start()
    scale_load.start()
    for n in (1, 2, 3, 0):
        panel_loads[n].start()
    rhs_load.start()
    own_load.wait()
    value_high, value_low = split(mine[...])
    x = []
    for n, rows in enumerate(parts):
        inverse_loads[n].wait()
        high_part, low_part = split(inverse[rows, :])
        high[rows, :], low[rows, :] = high_part, low_part
        part = dot(high_part, value_high) + dot(high_part, value_low)
        x.append((part + dot(low_part, value_high)).astype(BF16))
    x = jnp.concatenate(x, axis=0)
    scale_load.wait()
    for n in range(CHAINS):
        scales[n : n + 1, :] = jnp.full((1, RHS), numbers[n], F32)
    panel_loads[1].wait()
    u1[...] = tile(scales, panel, 1, x)
    for n in (2, 3):
        panel_loads[n].wait()
        u23[(n - 2) * BLOCK : (n - 1) * BLOCK, :] = tile(scales, panel, n, x).astype(BF16)
    panel_loads[0].wait()
    rhs_load.wait()


def bridge(scales, high, low, panel, out):
    last = panel[3 * BLOCK :, :]
    product = dot(last, high[...]) + dot(last, low[...])
    out[...] = (scales[3:4, :1] * product).astype(BF16)


def second(scales, rhs, high, low, panel, m1, s1, solved, r2, r3):
    x = product(high, low, own(rhs) - m1[...]).astype(BF16)
    solved[...] = x
    for n, ref in ((2, r2), (3, r3)):
        rows = slice(n * BLOCK, (n + 1) * BLOCK)
        past = s1[(n - 2) * BLOCK : (n - 1) * BLOCK, :].astype(F32)
        ref[...] = rhs[rows, :] - past - tile(scales, panel, n, x)


def across(r2, r3, bridged, out):
    high, low = split(r2[...])
    out[...] = r3[...] - dot(bridged[...], high) - dot(bridged[...], low)


def third(rhs, high, low, m1, m2, relayed, solved):
    value = jnp.where(chain_index() == 2, m2[...], own(rhs) - m1[...])
    x = product(high, low, value).astype(BF16).astype(F32)
    keep = is_head() & (chain_index() < CHAINS - 1)
    solved[...] = (jnp.where(keep, x, 0.0) + relayed[...].astype(F32)).astype(BF16)


def fourth(high, low, ra, rb, rc, solved, xa, xb, xc, out):
    x = product(high, low, ra[...] + rb[...] + rc[...])
    for part in (solved, xa, xb, xc):
        x = x + part[...].astype(F32)
    out[...] = x.astype(BF16)


def update(scales, panel, x, kept, ahead2, ahead1, ahead3):
    for ref, shift in ((ahead2, 2), (ahead1, 1), (ahead3, 3), (kept, 0)):
        i = lax.rem(chain_index() + shift, CHAINS)
        ref[...] = (scales[pl.ds(i, 1), :] * dot(panel[block(i), :], x[...])).astype(ref.dtype)


def total(x, kept, a2, a1, a3, out):
    summed = kept[...] + a2[...].astype(F32) + a1[...].astype(F32) + a3[...].astype(F32)
    out[...] = jnp.where(is_head(), -x[...].astype(F32), summed).astype(BF16)


def finish(rhs, mine, b2, b1, b3, out, stage, sems):
    head = is_head()
    copies = []
    for n, (ref, shift) in enumerate(((mine, 0), (b2, 2), (b1, 1), (b3, 3))):
        i = lax.rem(chain_index() + CHAINS - shift, CHAINS)
        rows = block(i)
        stage[n] = jnp.where(head, 0.0, rhs[rows, :]) - ref[...].astype(F32)
        copy = pltpu.make_async_copy(stage.at[n], out.at[rows, :], sems.at[n])
        copy.start()
        copies.append(copy)
    for copy in copies:
        copy.wait()


def both_cores(value):
    return lax.all_gather(value, "row", axis_index_groups=CORE_PAIRS)[0]


def send(value, pairs):
    return lax.ppermute(value, ("chain", "row"), pairs)


def local(right_side, factor, tile_scales, diag_inverse):
    scales = tile_scales.reshape(CHAINS)
    panel = factor.reshape(factor.shape[0], factor.shape[2])
    inverse = diag_inverse[0]
    root = CENTRES[0]

    right, panel, high, low, scales, u1, u23 = call(
        first,
        (
            pltpu.VMEM(right_side.shape, F32),
            pltpu.VMEM(panel.shape, BF16),
            pltpu.VMEM((BLOCK, BLOCK), BF16),
            pltpu.VMEM((BLOCK, BLOCK), BF16),
            pltpu.VMEM((CHAINS, RHS), F32),
            COLUMN,
            pltpu.VMEM((2 * BLOCK, RHS), BF16),
        ),
        [HBM] * 4,
        scales, right_side, inverse, panel,
        scratch=[
            pltpu.VMEM((BLOCK, BLOCK), F32),
            pltpu.VMEM((BLOCK, RHS), F32),
            pltpu.SMEM((CHAINS,), F32),
            pltpu.SemaphoreType.DMA((3 + CHUNKS + CHAINS,)),
        ],
    )
    m1 = send(u1, [(device_of(0, root), device_of(1, root))])
    s1 = send(u23, [(device_of(0, root), device_of(1, root))])
    bridged = call(bridge, pltpu.VMEM((BLOCK, BLOCK), BF16), [VMEM] * 4, scales, high, low, panel)
    bridged = send(bridged, [(device_of(2, root), device_of(1, root))])
    solved, r2, r3 = call(
        second,
        (LOW, COLUMN, COLUMN),
        [VMEM] * 7,
        scales, right, high, low, panel, m1, s1,
    )
    m2 = send(r2, [(device_of(1, root), device_of(2, root))])
    relayed = send(solved, [(device_of(1, root), device_of(1, RELAY))])
    residue = both_cores(call(across, COLUMN, [VMEM] * 3, r2, r3, bridged))
    r = [
        send(residue, [(device_of(1, a, core), device_of(3, b)) for a, core, b in step])
        for step in fan_out({root: CENTRES})
    ]
    solved = call(third, LOW, [VMEM] * 6, right, high, low, m1, m2, relayed)
    solved = both_cores(solved)
    inside = [
        fan_out({root: CENTRES[1:]}),
        fan_out({RELAY: [c for c in CENTRES[1:] if c != RELAY]}),
        fan_out({root: CENTRES[1:]}),
    ]
    s = []
    for n in range(3):
        pairs = [
            (device_of(k, a, core), device_of(k, b))
            for k, steps in enumerate(inside)
            for a, core, b in (steps[n] if n < len(steps) else [])
        ]
        s.append(send(solved, pairs))
    x = call(fourth, LOW, [VMEM] * 9, high, low, *r, solved, *s)
    x = both_cores(x)
    got = [
        lax.ppermute(x, "row", [(row_of(a, core), row_of(b)) for a, core, b in pairs])
        for pairs in fan_out(TREE)
    ]
    x = both_cores(sum(got, x))

    kept, *ahead = call(update, (COLUMN, LOW, LOW, LOW), [VMEM] * 3, scales, panel, x)

    def ring(value, shift):
        pairs = [(j, (j + shift) % CHAINS) for j in range(CHAINS)]
        return lax.ppermute(value, "chain", pairs)

    arrived = [ring(a, s) for a, s in zip(ahead, (2, 1, 3))]
    mine = call(total, LOW, [VMEM] * 5, x, kept, *arrived)
    theirs = [ring(mine, s) for s in (2, 1, 3)]
    return pl.pallas_call(
        finish,
        out_shape=jax.ShapeDtypeStruct(right_side.shape, F32),
        in_specs=[VMEM] * 5,
        out_specs=HBM,
        scratch_shapes=[
            pltpu.VMEM((CHAINS, BLOCK, RHS), F32),
            pltpu.SemaphoreType.DMA((CHAINS,)),
        ],
        compiler_params=pltpu.CompilerParams(vmem_limit_bytes=KERNEL_VMEM),
    )(on_chip(right), on_chip(mine), *map(on_chip, theirs))


def solution(mesh):
    return jax.shard_map(
        local,
        mesh=mesh,
        in_specs=(
            P("row", None),
            P("row", None, "chain"),
            P("row", None, "chain"),
            P(None, None, "chain"),
        ),
        out_specs=P("row", None),
        check_vma=False,
    )
```

```python
import jax
import jax.numpy as jnp
from jax import lax
from jax.experimental import pallas as pl
from jax.experimental.pallas import tpu as pltpu
from jax.sharding import PartitionSpec as P


BF16 = jnp.bfloat16
F32 = jnp.float32
BLOCK = 512
RHS = 128
CHAINS = 4
ROWS = 64
CHIPS = (4, 8)
KERNEL_VMEM = 12 * 1024 * 1024

TREE = {
    (0, 0): ((0, 7), (1, 0), (1, 7), (3, 0), (3, 7)),
    (2, 1): ((1, 1), (2, 0), (2, 2), (3, 1)),
    (1, 3): ((0, 3), (1, 4), (2, 3), (2, 4)),
    (2, 6): ((1, 6), (2, 5), (2, 7), (3, 6)),
    (0, 2): ((0, 1), (1, 2), (3, 2), (3, 3)),
    (0, 5): ((0, 4), (0, 6), (1, 5), (3, 4), (3, 5)),
}
CENTRES = tuple(TREE)
RELAY = (1, 3)
CORE_PAIRS = [[2 * i, 2 * i + 1] for i in range(ROWS // 2)]

VMEM = pl.BlockSpec(memory_space=pltpu.VMEM)
HBM = pl.BlockSpec(memory_space=pltpu.HBM)
COLUMN = pltpu.VMEM((BLOCK, RHS), F32)
LOW = pltpu.VMEM((BLOCK, RHS), BF16)


def row_of(chip, core=0):
    return chip[0] * 16 + chip[1] * 2 + core


def device_of(chain, chip, core=0):
    return chain * ROWS + row_of(chip, core)


def hops(a, b):
    return sum(min((p - q) % n, (q - p) % n) for p, q, n in zip(a, b, CHIPS))


def fan_out(tree):
    rounds = max((len(leaves) + 1) // 2 for leaves in tree.values())
    steps = [[] for _ in range(rounds)]
    for chip, leaves in tree.items():
        for i, leaf in enumerate(sorted(leaves, key=lambda b: -hops(chip, b))):
            steps[i // 2].append((chip, i % 2, leaf))
    return steps


def on_chip(value):
    return pltpu.with_memory_space_constraint(value, pltpu.VMEM)


def call(body, outs, specs, *args, scratch=()):
    args = [
        pltpu.with_memory_space_constraint(a, s.memory_space) for a, s in zip(args, specs)
    ]
    single = not isinstance(outs, tuple)
    return pl.pallas_call(
        body,
        out_shape=outs,
        in_specs=specs,
        out_specs=VMEM if single else (VMEM,) * len(outs),
        scratch_shapes=scratch,
        compiler_params=pltpu.CompilerParams(vmem_limit_bytes=KERNEL_VMEM),
    )(*args)


def dot(a, b):
    return jnp.dot(a, b, preferred_element_type=F32)


def split(value):
    high = value.astype(BF16)
    return high, (value - high.astype(F32)).astype(BF16)


def wide(value):
    return jnp.concatenate(split(value), axis=1)


def product(halves, value):
    full = dot(halves[...], wide(value))
    return full[:BLOCK, :RHS] + full[:BLOCK, RHS:] + full[BLOCK:, :RHS] + full[BLOCK:, RHS:]


def chain_index():
    return lax.axis_index("chain")


def is_head():
    return lax.axis_index("row") == 0


def block(i):
    return pl.ds(pl.multiple_of(i * BLOCK, BLOCK), BLOCK)


def own(ref):
    return ref[block(chain_index()), :]


def tiles(scales, panel, start, solved_low):
    full = dot(panel[start * BLOCK :, :], solved_low)
    return [
        scales[i : i + 1, :] * full[(i - start) * BLOCK : (i - start + 1) * BLOCK, :]
        for i in range(start, CHAINS)
    ]


def first(
    scales_in, rhs_in, inverse_in, panel_in, rhs, panel, halves, scales, u, r1, inverse, mine, numbers, sems
):
    head, rest = pl.ds(0, BLOCK), pl.ds(BLOCK, 3 * BLOCK)
    loads = [
        pltpu.make_async_copy(source, target, sems.at[n])
        for n, (source, target) in enumerate(
            (
                (inverse_in, inverse),
                (rhs_in.at[block(chain_index()), :], mine),
                (scales_in, numbers),
                (panel_in.at[rest, :], panel.at[rest, :]),
                (panel_in.at[head, :], panel.at[head, :]),
                (rhs_in, rhs),
            )
        )
    ]
    for load in loads:
        load.start()
    loads[0].wait()
    halves[:BLOCK, :], halves[BLOCK:, :] = split(inverse[...])
    loads[1].wait()
    x = product(halves, mine[...]).astype(BF16)
    loads[2].wait()
    for n in range(CHAINS):
        scales[n : n + 1, :] = jnp.full((1, RHS), numbers[n], F32)
    loads[3].wait()
    for n, part in enumerate(tiles(scales, panel, 1, x)):
        u[n * BLOCK : (n + 1) * BLOCK, :] = part.astype(BF16)
        if n == 0:
            first_part = part
    for load in loads[4:]:
        load.wait()
    r1[...] = rhs[BLOCK : 2 * BLOCK, :] - first_part


def bridge(scales, halves, panel, out):
    last = panel[3 * BLOCK :, :]
    full = dot(last, halves[:BLOCK, :]) + dot(last, halves[BLOCK:, :])
    out[...] = (scales[3:4, :1] * full).astype(BF16)


def past(m1, n):
    return m1[(n - 1) * BLOCK : n * BLOCK, :].astype(F32)


def second(scales, rhs, halves, panel, m1, solved, r2):
    x = product(halves, own(rhs) - past(m1, 1)).astype(BF16)
    solved[...] = x
    part = scales[2:3, :] * dot(panel[2 * BLOCK : 3 * BLOCK, :], x)
    r2[...] = (rhs[2 * BLOCK : 3 * BLOCK, :] - past(m1, 2) - part).astype(r2.dtype)


def across(scales, rhs, panel, m1, solved, r2, bridged, out):
    part = scales[3:4, :] * dot(panel[3 * BLOCK :, :], solved[...])
    r3 = rhs[3 * BLOCK :, :] - past(m1, 3) - part
    full = dot(bridged[...], wide(r2[...]))
    out[...] = (r3 - full[:, :RHS] - full[:, RHS:]).astype(out.dtype)


def third(rhs, halves, m1, m2, relayed, solved):
    chain, row = chain_index(), lax.axis_index("row")
    value = jnp.where(chain == 2, m2[...], own(rhs) - past(m1, 1))
    relay = row == row_of(RELAY)
    x = product(halves, jnp.where(relay, relayed[...], value))
    keep = (is_head() & (chain < CHAINS - 1)) | (relay & (chain == 1))
    solved[...] = jnp.where(keep, x, 0.0).astype(BF16)


def fourth(halves, ra, rb, rc, solved, xa, xb, xc, out):
    x = product(halves, ra[...].astype(F32) + rb[...].astype(F32) + rc[...].astype(F32))
    for part in (solved, xa, xb, xc):
        x = x + part[...].astype(F32)
    out[...] = x.astype(BF16)


def update(scales, panel, x, ahead2, ahead1, ahead3, kept, full):
    full[...] = dot(panel[...], x[...])
    for ref, shift in ((ahead2, 2), (ahead1, 1), (ahead3, 3), (kept, 0)):
        i = lax.rem(chain_index() + shift, CHAINS)
        ref[...] = (scales[pl.ds(i, 1), :] * full[block(i), :]).astype(ref.dtype)


def total(x, kept, a1, a3, a2, out):
    summed = kept[...] + a2[...].astype(F32) + a1[...].astype(F32) + a3[...].astype(F32)
    out[...] = jnp.where(is_head(), -x[...].astype(F32), summed).astype(BF16)


def finish(rhs, mine, b1, b3, b2, out, stage, sems):
    head = is_head()
    copies = []
    for n, (ref, shift) in enumerate(((mine, 0), (b1, 1), (b3, 3), (b2, 2))):
        i = lax.rem(chain_index() + CHAINS - shift, CHAINS)
        rows = block(i)
        stage[n] = jnp.where(head, 0.0, rhs[rows, :]) - ref[...].astype(F32)
        copy = pltpu.make_async_copy(stage.at[n], out.at[rows, :], sems.at[n])
        copy.start()
        copies.append(copy)
    for copy in copies:
        copy.wait()


def both_cores(value):
    return lax.all_gather(value, "row", axis_index_groups=CORE_PAIRS)[0]


def send(value, pairs):
    return lax.ppermute(value, ("chain", "row"), pairs)


def local(right_side, factor, tile_scales, diag_inverse):
    scales = tile_scales.reshape(CHAINS)
    panel = factor.reshape(factor.shape[0], factor.shape[2])
    inverse = diag_inverse[0]
    root = CENTRES[0]

    right, panel, halves, scales, u, r1 = call(
        first,
        (
            pltpu.VMEM(right_side.shape, F32),
            pltpu.VMEM(panel.shape, BF16),
            pltpu.VMEM((2 * BLOCK, BLOCK), BF16),
            pltpu.VMEM((CHAINS, RHS), F32),
            pltpu.VMEM((3 * BLOCK, RHS), BF16),
            COLUMN,
        ),
        [HBM] * 4,
        scales, right_side, inverse, panel,
        scratch=[
            pltpu.VMEM((BLOCK, BLOCK), F32),
            pltpu.VMEM((BLOCK, RHS), F32),
            pltpu.SMEM((CHAINS,), F32),
            pltpu.SemaphoreType.DMA((6,)),
        ],
    )
    m1 = send(u, [(device_of(0, root), device_of(1, root))])
    bridged = call(
        bridge, pltpu.VMEM((BLOCK, BLOCK), BF16), [VMEM] * 3, scales, halves, panel
    )
    bridged = send(bridged, [(device_of(2, root), device_of(1, root))])
    relayed = send(r1, [(device_of(0, root), device_of(1, RELAY))])
    solved, r2 = call(
        second, (LOW, COLUMN), [VMEM] * 5, scales, right, halves, panel, m1
    )
    m2 = send(r2, [(device_of(1, root), device_of(2, root))])
    residue = call(across, LOW, [VMEM] * 7, scales, right, panel, m1, solved, r2, bridged)
    residue = both_cores(residue)
    r = [
        send(residue, [(device_of(1, a, core), device_of(3, b)) for a, core, b in step])
        for step in fan_out({root: CENTRES})
    ]
    solved = call(third, LOW, [VMEM] * 5, right, halves, m1, m2, relayed)
    solved = both_cores(solved)
    inside = [
        fan_out({root: CENTRES[1:]}),
        fan_out({RELAY: [c for c in CENTRES[1:] if c != RELAY]}),
        fan_out({root: CENTRES[1:]}),
    ]
    s = []
    for n in range(3):
        pairs = [
            (device_of(k, a, core), device_of(k, b))
            for k, steps in enumerate(inside)
            for a, core, b in (steps[n] if n < len(steps) else [])
        ]
        s.append(send(solved, pairs))
    x = call(fourth, LOW, [VMEM] * 8, halves, *r, solved, *s)
    x = both_cores(x)
    got = []
    for step in fan_out(TREE):
        pairs = [
            (device_of(k, a, core), device_of(k, b)) for k in range(CHAINS) for a, core, b in step
        ]
        got.append(send(x, pairs))
    x = both_cores(sum(got, x))

    ahead2, ahead1, ahead3, kept = call(
        update,
        (LOW, LOW, LOW, COLUMN),
        [VMEM] * 3,
        scales, panel, x,
        scratch=[pltpu.VMEM(panel.shape[:1] + (RHS,), F32)],
    )

    def ring(value, shift):
        pairs = [(j, (j + shift) % CHAINS) for j in range(CHAINS)]
        return lax.ppermute(value, "chain", pairs)

    arrived = [ring(a, s) for a, s in ((ahead1, 1), (ahead3, 3), (ahead2, 2))]
    mine = call(total, LOW, [VMEM] * 5, x, kept, *arrived)
    theirs = [ring(mine, s) for s in (1, 3, 2)]
    return pl.pallas_call(
        finish,
        out_shape=jax.ShapeDtypeStruct(right_side.shape, F32),
        in_specs=[VMEM] * 5,
        out_specs=HBM,
        scratch_shapes=[
            pltpu.VMEM((CHAINS, BLOCK, RHS), F32),
            pltpu.SemaphoreType.DMA((CHAINS,)),
        ],
        compiler_params=pltpu.CompilerParams(vmem_limit_bytes=KERNEL_VMEM),
    )(on_chip(right), on_chip(mine), *map(on_chip, theirs))


def solution(mesh):
    return jax.shard_map(
        local,
        mesh=mesh,
        in_specs=(
            P("row", None),
            P("row", None, "chain"),
            P("row", None, "chain"),
            P(None, None, "chain"),
        ),
        out_specs=P("row", None),
        check_vma=False,
    )
```
